256 devices in a mesh: row: 16 (over y_hi, z), col: 16 (over y_lo, x, core).
Axes of the slice: x: 4, y: 4 (y_hi: 2, y_lo: 2; y = y_hi * 2 + y_lo), z: 8, core: 2. Of those that a mesh axis runs over, the one named last changes fastest.
Arguments:
- obs_panel: bfloat16 [196608, 2048], P('row', 'col'), may hold values from -0.1875 to 0.1875
- skies: bfloat16 [196608, 256], P('row', 'col'), may hold values from -6 to 6
- panel_index: int32 [2048], replicated, may hold values from 0 to 196607
- prior_sum: float32 [196608, 256], P('row', 'col'), may hold values from -6 to 6
- apod: float32 [196608], P('row'), may hold values from 0.05 to 1
- proj_panel: bfloat16 [2048, 196608], P(None, ('row', 'col')), may hold values from -0.0546875 to 0.0546875
Outputs:
- reobserved: float32 [196608, 256], P('row', 'col')
- projection: float32 [2048, 256], P('row', 'col')
The draws below stay inside these ranges and needn't reach their ends.
Inputs may be any that keep to these rules, and one draw needn't show every extreme that they name: `panel_index`: rows of the observed patch; a row may appear more than once.
All inputs are finite; a program needn't handle non-finite values.
Results may differ from the reference program's by a relative error of at most 0.0029.
Values may be sent and summed in bfloat16 or wider, within the bound.
No kernel may reach another device: no remote copies, remote signals or barrier semaphores. Data moves between devices by JAX's collectives and lax.ppermute only.
A program may use at most 64 MiB of HBM per device.

```python
import math
import jax
import jax.numpy as jnp

NP = 196608
PANEL = 2048
NSIM = 256
PROWS = 2048


def set_ends(array, own_key, least, top_value):
    spot = [jax.random.randint(jax.random.fold_in(own_key, axis), (), 0, length) for axis, length in enumerate(array.shape)]
    longest = array.shape.index(max(array.shape))
    next_to = spot[:longest] + [(spot[longest] + 1) % array.shape[longest]] + spot[longest + 1:]
    return array.at[tuple(spot)].set(least).at[tuple(next_to)].set(top_value)


def with_spikes(entries, own_key, source, target, parts, factor):
    owner, partner = [(jnp.arange(entries.shape[dim]) // (entries.shape[dim] // parts)).reshape([-1 if axis == dim else 1 for axis in range(entries.ndim)]) for dim in (source, target)]
    chosen = jax.random.permutation(own_key, parts)[partner]
    strong = (owner == chosen) | (owner == (partner + parts // 2) % parts)
    return jnp.where(strong, factor * entries, entries)


def block_scale(key, dims, shards, low, largest):
    loudness, own = 1.0, jax.random.fold_in(key, 6)
    for axis_at, blocks in shards:
        steps = jnp.exp(jax.random.uniform(jax.random.fold_in(own, axis_at), (blocks,), jnp.float32, low / len(shards), largest / len(shards)))
        loudness = loudness * jnp.repeat(steps, dims[axis_at] // blocks).reshape([-1 if axis == axis_at else 1 for axis in range(len(dims))])
    return loudness


def bell_draw(own_key, dims, deviation, bound, split=(), dtype=jnp.bfloat16):
    result = jax.random.normal(own_key, dims, jnp.float32) * deviation
    if len(split) > 0:
        result = block_scale(own_key, dims, split, -0.22, 0.18) * result
    return jnp.clip(result, min=-bound, max=bound).astype(dtype)


def gaussian_with(own_key, extent, width, most, pieces, heavy, held_as=jnp.bfloat16):
    values = width * jax.random.normal(own_key, extent, jnp.float32)
    if pieces:
        values = values * block_scale(own_key, extent, pieces, -0.22, 0.18)
    return jnp.clip(with_spikes(values, jax.random.fold_in(own_key, 3), *heavy), -most, most).astype(held_as)


def setup_inputs(seed: int = 0) -> dict:
    arg_keys = jax.random.split(jax.random.key(seed), 7)
    return {
        "obs_panel": gaussian_with(arg_keys[0], (NP, PANEL), PANEL ** -0.5, 0.1875, ((0, 16), (1, 16)), (1, 0, 16, 2.0)),
        "skies": bell_draw(arg_keys[1], (NP, NSIM), 1.0, 6.0, ((0, 16), (1, 16))),
        "panel_index": set_ends(jax.random.randint(arg_keys[2], (PANEL,), 0, NP), jax.random.fold_in(arg_keys[2], 1), 0, NP - 1).astype(jnp.int32),
        "prior_sum": bell_draw(arg_keys[3], (NP, NSIM), 1.0, 6.0, ((0, 16), (1, 16)), jnp.float32),
        "apod": jnp.clip(jnp.exp(math.log(1.0) - 2.9957323 * jax.random.uniform(arg_keys[4], (NP,), jnp.float32) ** block_scale(arg_keys[4], (NP,), ((0, 16),), -0.2, 0.2)), 0.05, 1.0),
        "proj_panel": gaussian_with(arg_keys[5], (PROWS, NP), NP ** -0.5, 0.0546875, ((1, 256),), (1, 0, 256, 6.0)),
    }


def reference(obs_panel, skies, panel_index, prior_sum, apod, proj_panel):
    picked = jnp.take(skies, panel_index, axis=0)
    reobserved = prior_sum + jnp.dot(obs_panel, picked, preferred_element_type=jnp.float32)
    weighted = (apod[:, None] * reobserved).astype(jnp.bfloat16)
    projection = jnp.dot(proj_panel, weighted, preferred_element_type=jnp.float32)
    return reobserved, projection
```

```python
import jax
import jax.numpy as jnp
from jax import lax
from jax.experimental import pallas as pl
from jax.experimental.pallas import tpu as pltpu
from jax.sharding import PartitionSpec as P

F32, BF16 = jnp.float32, jnp.bfloat16
LANES = 128


def pick_kernel(first_ref, idx_ref, sky_ref, out_ref):
    evo, rows = sky_ref.shape
    groups = rows // LANES
    local = idx_ref[...] - first_ref[0]
    lane = lax.broadcasted_iota(jnp.int32, (LANES, local.shape[1]), 0)
    onehot = jnp.where(lane == (local & (LANES - 1)), 1.0, 0.0).astype(BF16)
    group = lax.shift_right_arithmetic(local, 7)
    total = jnp.zeros(out_ref.shape, F32)
    step = 16
    for start in range(0, groups, step):
        block = jnp.concatenate(
            [sky_ref[:, g * LANES : (g + 1) * LANES] for g in range(start, start + step)], axis=0
        )
        found = jnp.dot(block, onehot, preferred_element_type=F32)
        for g in range(step):
            total = total + jnp.where(group == start + g, found[g * evo : (g + 1) * evo], 0.0)
    out_ref[...] = total.astype(BF16)


def pick(first, idx, sky):
    evo, rows = sky.shape
    count = idx.shape[1]
    tile = 256
    return pl.pallas_call(
        pick_kernel,
        out_shape=jax.ShapeDtypeStruct((evo, count), BF16),
        grid_spec=pltpu.PrefetchScalarGridSpec(
            num_scalar_prefetch=1,
            grid=(count // tile,),
            in_specs=[
                pl.BlockSpec((1, tile), lambda i, _: (0, i)),
                pl.BlockSpec((evo, rows), lambda i, _: (0, 0)),
            ],
            out_specs=pl.BlockSpec((evo, tile), lambda i, _: (0, i)),
        ),
        cost_estimate=pl.CostEstimate(
            flops=2 * evo * rows * count, bytes_accessed=2 * evo * rows + 2 * evo * count, transcendentals=0
        ),
    )(first, idx, sky)


def gather(x, axis, n):
    return lax.all_to_all(jnp.broadcast_to(x[None], (n, *x.shape)), axis, 0, 0, tiled=True)


def on_device(n_row, n_col, obs, skies, idx, prior, apod, proj):
    rows_blk, evo = skies.shape
    sub = rows_blk // n_col
    count = idx.shape[0]
    first = (lax.axis_index("row") * rows_blk).astype(jnp.int32)
    picked = pick(first.reshape(1), idx.reshape(1, count), skies.T)
    shares = lax.all_to_all(picked.reshape(evo, n_row, count // n_row), "row", 1, 0, tiled=True)
    shares = shares.reshape(n_row, evo, count // n_row).astype(F32).sum(0).astype(BF16)
    mine = gather(shares, "row", n_row).transpose(1, 0, 2).reshape(evo, count)
    panel = gather(mine, "col", n_col).reshape(n_col * evo, count)

    obs_rows = lax.all_to_all(obs, "col", 0, 1, tiled=True)
    prior_t = prior.T
    prior_rows = lax.all_to_all(prior_t, "col", 1, 0, tiled=True)

    added = lax.dot_general(panel, obs_rows, (((1,), (1,)), ((), ())), preferred_element_type=F32)
    apod_sub = lax.dynamic_slice(apod, (lax.axis_index("col") * sub,), (sub,))
    reob = prior_rows + added
    weighted = (apod_sub[None, :] * reob).astype(BF16)
    partial = lax.dot_general(weighted, proj, (((1,), (1,)), ((), ())), preferred_element_type=F32)
    shared = lax.all_to_all(partial.astype(BF16).reshape(n_col, evo, -1), "col", 0, 0, tiled=True)
    column = shared.astype(F32).sum(0)
    column = lax.all_to_all(column.reshape(evo, n_row, -1), "row", 1, 0, tiled=True)
    projection = column.reshape(n_row, evo, -1).sum(0).T

    back = lax.all_to_all(added, "col", 0, 1, tiled=True)
    reobserved = (prior_t + back).T
    return reobserved, projection


def solution(mesh):
    n_row, n_col = mesh.shape["row"], mesh.shape["col"]

    def step(*args):
        return on_device(n_row, n_col, *args)

    return jax.shard_map(
        step,
        mesh=mesh,
        in_specs=(P("row", "col"), P("row", "col"), P(), P("row", "col"), P("row"), P(None, ("row", "col"))),
        out_specs=(P("row", "col"), P("row", "col")),
        check_vma=False,
    )
```

```python
import functools

import jax
import jax.numpy as jnp
from jax import lax
from jax.experimental import pallas as pl
from jax.experimental.pallas import tpu as pltpu
from jax.sharding import PartitionSpec as P

F32, BF16 = jnp.float32, jnp.bfloat16
LANES = 128
WIDE = 256
MIB = 1 << 20
NT = (((1,), (1,)), ((), ()))


def whole(n):
    return [pl.BlockSpec(memory_space=pltpu.VMEM)] * n


def cost(flops, nbytes):
    return pl.CostEstimate(flops=flops, bytes_accessed=nbytes, transcendentals=0)


def pack_kernel(dests, obs_ref, prior_ref, out_ref):
    sub = obs_ref.shape[0] // dests
    evo = prior_ref.shape[0]
    for d in range(dests):
        out_ref[d, :sub] = obs_ref[d * sub : (d + 1) * sub]
        for l in range(sub // LANES):
            at = d * sub + l * LANES
            value = prior_ref[:, at : at + LANES]
            high = value.astype(BF16)
            row = sub + l * 2 * evo
            out_ref[d, row : row + evo] = high
            out_ref[d, row + evo : row + 2 * evo] = (value - high.astype(F32)).astype(BF16)


def pack(obs, prior_t, n_col):
    rows, width = obs.shape
    evo = prior_t.shape[0]
    sub = rows // n_col
    depth = sub + 2 * evo * sub // LANES
    dests = 4
    return pl.pallas_call(
        functools.partial(pack_kernel, dests),
        out_shape=jax.ShapeDtypeStruct((n_col, depth, width), BF16),
        grid=(n_col // dests,),
        in_specs=[
            pl.BlockSpec((dests * sub, width), lambda i: (i, 0)),
            pl.BlockSpec((evo, dests * sub), lambda i: (0, i)),
        ],
        out_specs=pl.BlockSpec((dests, depth, width), lambda i: (i, 0, 0)),
        cost_estimate=cost(0, 2 * 2 * n_col * depth * width),
    )(obs, prior_t)


def pick_kernel(first_ref, idx_ref, sky_ref, out_ref):
    evo, rows = sky_ref.shape
    groups = rows // WIDE
    local = idx_ref[...] - first_ref[0]
    place = lax.broadcasted_iota(jnp.int32, (WIDE, local.shape[1]), 0)
    onehot = jnp.where(place == (local & (WIDE - 1)), 1.0, 0.0).astype(BF16)
    group = lax.shift_right_arithmetic(local, WIDE.bit_length() - 1)
    total = jnp.zeros(out_ref.shape, F32)
    step = 16
    for start in range(0, groups, step):
        block = jnp.concatenate(
            [sky_ref[:, g * WIDE : (g + 1) * WIDE] for g in range(start, start + step)], axis=0
        )
        found = jnp.dot(block, onehot, preferred_element_type=F32)
        for g in range(step):
            total = total + jnp.where(group == start + g, found[g * evo : (g + 1) * evo], 0.0)
    out_ref[...] = total.astype(BF16)


def pick(first, idx, sky):
    evo, rows = sky.shape
    count = idx.shape[1]
    tile = 512
    return pl.pallas_call(
        pick_kernel,
        out_shape=jax.ShapeDtypeStruct((evo, count), BF16),
        grid_spec=pltpu.PrefetchScalarGridSpec(
            num_scalar_prefetch=1,
            grid=(count // tile,),
            in_specs=[
                pl.BlockSpec((1, tile), lambda i, _: (0, i)),
                pl.BlockSpec((evo, rows), lambda i, _: (0, 0)),
            ],
            out_specs=pl.BlockSpec((evo, tile), lambda i, _: (0, i)),
        ),
        cost_estimate=cost(2 * evo * rows * count, 2 * evo * rows + 2 * evo * count),
    )(first, idx, sky)


def main_kernel(
    me_ref, msg_ref, own_ref, other_ref, apod_ref, proj_ref, p_own, p_other, s_own, s_other, panel, weighted
):
    chips, evo, count = own_ref.shape
    prows, sub = proj_ref.shape
    me = me_ref[0]
    core = me % 2
    half = chips * evo
    for m in range(chips):
        panel[m * evo : (m + 1) * evo] = own_ref[m]
        panel[half + m * evo : half + (m + 1) * evo] = other_ref[m]
    sources = [2 * m + jnp.bitwise_xor(core, b) for b in range(2) for m in range(chips)]
    for n in range(sub // WIDE):
        rows = slice(n * WIDE, (n + 1) * WIDE)
        added = jnp.zeros((2 * half, WIDE), F32)
        for k in range(chips):
            obs = jnp.concatenate([msg_ref[2 * k, rows], msg_ref[2 * k + 1, rows]], axis=1)
            added += lax.dot_general(
                panel[:, k * WIDE : (k + 1) * WIDE], obs, NT, preferred_element_type=F32
            )
        s_own[:, :, rows] = added[:half].astype(BF16).reshape(chips, evo, WIDE)
        s_other[:, :, rows] = added[half:].astype(BF16).reshape(chips, evo, WIDE)
        for l in range(WIDE // LANES):
            block = n * (WIDE // LANES) + l
            row = sub + block * 2 * evo
            prior = jnp.concatenate(
                [
                    msg_ref[s, row : row + evo].astype(F32) + msg_ref[s, row + evo : row + 2 * evo].astype(F32)
                    for s in sources
                ],
                axis=0,
            )
            weight = apod_ref[pl.ds(me * (sub // LANES) + block, 1), :]
            value = weight * (prior + added[:, l * LANES : (l + 1) * LANES])
            weighted[:, block * LANES : (block + 1) * LANES] = value.astype(BF16)
    for n in range(prows // WIDE):
        cols = slice(n * WIDE, (n + 1) * WIDE)
        part = lax.dot_general(weighted[...], proj_ref[cols], NT, preferred_element_type=F32)
        p_own[:, :, cols] = part[:half].reshape(chips, evo, WIDE)
        p_other[:, :, cols] = part[half:].reshape(chips, evo, WIDE)


def main_step(me, msg, own, other, apod, proj):
    chips, evo, count = own.shape
    prows, sub = proj.shape
    total = 2 * chips * evo
    return pl.pallas_call(
        main_kernel,
        out_shape=(
            jax.ShapeDtypeStruct((chips, evo, prows), F32),
            jax.ShapeDtypeStruct((chips, evo, prows), F32),
            jax.ShapeDtypeStruct((chips, evo, sub), BF16),
            jax.ShapeDtypeStruct((chips, evo, sub), BF16),
        ),
        in_specs=[pl.BlockSpec(memory_space=pltpu.SMEM)] + whole(5),
        out_specs=tuple(whole(4)),
        scratch_shapes=[pltpu.VMEM((total, count), BF16), pltpu.VMEM((total, sub), BF16)],
        compiler_params=pltpu.CompilerParams(vmem_limit_bytes=28 * MIB),
        cost_estimate=cost(2 * total * sub * (count + prows), 2 * msg.size + 2 * proj.size + 4 * total * prows),
    )(me, msg, own, other, apod, proj)


def home_kernel(p_own, p_got, s_own, s_got, out_ref):
    prows, sub = p_own.shape[2], s_own.shape[2]
    out_ref[:, :, :prows] = (p_own[...] + p_got[...]).astype(BF16)
    out_ref[:, :, prows : prows + sub] = s_own[...]
    out_ref[:, :, prows + sub :] = s_got[...]


def sum_kernel(msg_ref, out_ref):
    width = out_ref.shape[2]
    for n in range(out_ref.shape[0]):
        out_ref[n] = jnp.sum(msg_ref[:, :, n * width : (n + 1) * width].astype(F32), axis=0)


def add_kernel(prows, core_ref, msg_ref, prior_ref, out_ref):
    chips = msg_ref.shape[0]
    sub = prior_ref.shape[1] // (2 * chips)
    core = core_ref[0]
    for m in range(chips):
        for b in range(2):
            at = pl.ds(pl.multiple_of((2 * m + jnp.bitwise_xor(core, b)) * sub, LANES), sub)
            came = msg_ref[m, :, prows + b * sub : prows + (b + 1) * sub].astype(F32)
            out_ref[:, at] = prior_ref[:, at] + came


EARLY, LATE = (3, 5, 6, 7, 2), (1, 4)


def stack_kernel(*refs):
    for n, ref in enumerate(refs[:-1]):
        refs[-1][n] = ref[...]


def stack(parts):
    return pl.pallas_call(
        stack_kernel,
        out_shape=jax.ShapeDtypeStruct((len(parts), *parts[0].shape), parts[0].dtype),
        in_specs=whole(len(parts)),
        out_specs=whole(1)[0],
        cost_estimate=cost(0, 4 * len(parts) * parts[0].size),
    )(*parts)


def swap(x, axis, bits, n):
    return lax.ppermute(x, axis, [(i, i ^ bits) for i in range(n)])


def on_device(n_row, n_col, obs, skies, idx, prior, apod, proj):
    rows_blk, evo = skies.shape
    sub = rows_blk // n_col
    count = idx.shape[0]
    prows = proj.shape[0]
    chips = n_col // 2
    prior_t = prior.T
    me = lax.axis_index("col").astype(jnp.int32)
    first = (lax.axis_index("row") * rows_blk).astype(jnp.int32)
    picked = pick(first.reshape(1), idx.reshape(1, count), skies.T)
    far = swap(picked, "row", n_row // 2, n_row)
    packed, far = lax.optimization_barrier((pack(obs, prior_t, n_col), far))
    msg = lax.all_to_all(packed, "col", 0, 0, tiled=True)
    picked = picked + far
    for group in ((1, 2, 3), (4,)):
        parts = [swap(picked, "row", k, n_row) for k in group]
        for part in parts:
            picked = picked + part
    copies = jnp.broadcast_to(picked[None], (chips, evo, count))
    msg, copies = lax.optimization_barrier((msg, copies))
    same = [[2 * m + b for m in range(chips)] for b in range(2)]
    own = lax.all_to_all(copies, "col", 0, 0, tiled=True, axis_index_groups=same)
    other = swap(own, "col", 1, n_col)

    p_own, p_other, s_own, s_other = main_step(
        me.reshape(1), msg, own, other, apod.reshape(rows_blk // LANES, LANES), proj
    )
    p_got = swap(p_other, "col", 1, n_col)
    s_got = swap(s_other, "col", 1, n_col)
    home = pl.pallas_call(
        home_kernel,
        out_shape=jax.ShapeDtypeStruct((chips, evo, prows + 2 * sub), BF16),
        in_specs=whole(4),
        out_specs=whole(1)[0],
        compiler_params=pltpu.CompilerParams(vmem_limit_bytes=16 * MIB),
        cost_estimate=cost(p_own.size, 10 * p_own.size),
    )(p_own, p_got, s_own, s_got)
    same = [[2 * m + b for m in range(chips)] for b in range(2)]
    home = lax.all_to_all(home, "col", 0, 0, tiled=True, axis_index_groups=same)
    share = pl.pallas_call(
        sum_kernel,
        out_shape=jax.ShapeDtypeStruct((n_row, evo, prows // n_row), F32),
        in_specs=whole(1),
        out_specs=whole(1)[0],
        cost_estimate=cost(home.size, 2 * home.size),
    )(home)
    share = lax.all_to_all(share, "row", 0, 0, tiled=True)
    projection = share.sum(0).T
    reobserved = pl.pallas_call(
        functools.partial(add_kernel, prows),
        out_shape=jax.ShapeDtypeStruct((evo, rows_blk), F32),
        in_specs=[pl.BlockSpec(memory_space=pltpu.SMEM)] + whole(2),
        out_specs=whole(1)[0],
        cost_estimate=cost(prior.size, 10 * prior.size),
    )((me % 2).reshape(1), home, prior_t).T
    return reobserved, projection


def solution(mesh):
    n_row, n_col = mesh.shape["row"], mesh.shape["col"]
    return jax.shard_map(
        functools.partial(on_device, n_row, n_col),
        mesh=mesh,
        in_specs=(P("row", "col"), P("row", "col"), P(), P("row", "col"), P("row"), P(None, ("row", "col"))),
        out_specs=(P("row", "col"), P("row", "col")),
        check_vma=False,
    )
```

```python
import functools

import jax
import jax.numpy as jnp
from jax import lax
from jax.experimental import pallas as pl
from jax.experimental.pallas import tpu as pltpu
from jax.sharding import PartitionSpec as P

F32, BF16 = jnp.float32, jnp.bfloat16
LANES = 128
WIDE = 256
MIB = 1 << 20
NT = (((1,), (1,)), ((), ()))


def whole(n):
    return [pl.BlockSpec(memory_space=pltpu.VMEM)] * n


def cost(flops, nbytes):
    return pl.CostEstimate(flops=flops, bytes_accessed=nbytes, transcendentals=0)


def pack_kernel(chips, core_ref, obs_ref, prior_ref, keep_ref, give_ref):
    sub = obs_ref.shape[0] // (2 * chips)
    evo = prior_ref.shape[0]
    for m in range(chips):
        for side, out_ref in enumerate((keep_ref, give_ref)):
            start = pl.multiple_of((2 * m + jnp.bitwise_xor(core_ref[0], side)) * sub, LANES)
            out_ref[m, :sub] = obs_ref[pl.ds(start, sub)]
            for l in range(sub // LANES):
                value = prior_ref[:, pl.ds(pl.multiple_of(start + l * LANES, LANES), LANES)]
                high = value.astype(BF16)
                row = sub + l * 2 * evo
                out_ref[m, row : row + evo] = high
                out_ref[m, row + evo : row + 2 * evo] = (value - high.astype(F32)).astype(BF16)


def pack(core, obs, prior_t, n_col):
    rows, width = obs.shape
    evo = prior_t.shape[0]
    sub = rows // n_col
    depth = sub + 2 * evo * sub // LANES
    chips = 2
    block = pl.BlockSpec((chips, depth, width), lambda i, _: (i, 0, 0))
    return pl.pallas_call(
        functools.partial(pack_kernel, chips),
        out_shape=[jax.ShapeDtypeStruct((n_col // 2, depth, width), BF16)] * 2,
        grid_spec=pltpu.PrefetchScalarGridSpec(
            num_scalar_prefetch=1,
            grid=(n_col // 2 // chips,),
            in_specs=[
                pl.BlockSpec((2 * chips * sub, width), lambda i, _: (i, 0)),
                pl.BlockSpec((evo, 2 * chips * sub), lambda i, _: (0, i)),
            ],
            out_specs=[block] * 2,
        ),
        cost_estimate=cost(0, 2 * 2 * n_col * depth * width),
    )(core, obs, prior_t)


def join_kernel(got_ref, picked_ref, out_ref):
    chips, depth, width = got_ref.shape
    evo, count = picked_ref.shape
    out_ref[:, :depth] = got_ref[...]
    for l in range(count // width):
        tile = picked_ref[:, l * width : (l + 1) * width]
        for m in range(chips):
            out_ref[m, depth + l * evo : depth + (l + 1) * evo] = tile


def join(got, picked):
    chips, depth, width = got.shape
    more = picked.size // width
    return pl.pallas_call(
        join_kernel,
        out_shape=jax.ShapeDtypeStruct((chips, depth + more, width), BF16),
        grid=(chips // 2,),
        in_specs=[
            pl.BlockSpec((2, depth, width), lambda i: (i, 0, 0)),
            pl.BlockSpec(picked.shape, lambda i: (0, 0)),
        ],
        out_specs=pl.BlockSpec((2, depth + more, width), lambda i: (i, 0, 0)),
        cost_estimate=cost(0, 4 * chips * (depth + more) * width),
    )(got, picked)


def pick_kernel(first_ref, idx_ref, sky_ref, out_ref):
    evo, rows = sky_ref.shape
    groups = rows // WIDE
    local = idx_ref[...] - first_ref[0]
    place = lax.broadcasted_iota(jnp.int32, (WIDE, local.shape[1]), 0)
    onehot = jnp.where(place == (local & (WIDE - 1)), 1.0, 0.0).astype(BF16)
    group = lax.shift_right_arithmetic(local, WIDE.bit_length() - 1)
    total = jnp.zeros(out_ref.shape, F32)
    step = 16
    for start in range(0, groups, step):
        block = jnp.concatenate(
            [sky_ref[:, g * WIDE : (g + 1) * WIDE] for g in range(start, start + step)], axis=0
        )
        found = jnp.dot(block, onehot, preferred_element_type=F32)
        for g in range(step):
            total = total + jnp.where(group == start + g, found[g * evo : (g + 1) * evo], 0.0)
    out_ref[...] = total.astype(BF16)


def pick(first, idx, sky):
    evo, rows = sky.shape
    count = idx.shape[1]
    tile = 512
    return pl.pallas_call(
        pick_kernel,
        out_shape=jax.ShapeDtypeStruct((evo, count), BF16),
        grid_spec=pltpu.PrefetchScalarGridSpec(
            num_scalar_prefetch=1,
            grid=(count // tile,),
            in_specs=[
                pl.BlockSpec((1, tile), lambda i, _: (0, i)),
                pl.BlockSpec((evo, rows), lambda i, _: (0, 0)),
            ],
            out_specs=pl.BlockSpec((evo, tile), lambda i, _: (0, i)),
        ),
        cost_estimate=cost(2 * evo * rows * count, 2 * evo * rows + 2 * evo * count),
    )(first, idx, sky)


def main_kernel(
    me_ref, near_ref, far_ref, other_ref, apod_ref, proj_ref, p_own, p_other, s_own, s_other, panel, weighted
):
    chips, evo, _ = p_own.shape
    prows, sub = proj_ref.shape
    me = me_ref[0]
    core = me % 2
    half = chips * evo
    depth = near_ref.shape[1]
    for k in range(chips):
        for side in range(2):
            tile = (2 * k + jnp.bitwise_xor(core, side)) * evo
            lanes = slice((2 * k + side) * LANES, (2 * k + side + 1) * LANES)
            for m in range(chips):
                panel[m * evo : (m + 1) * evo, lanes] = far_ref[m, pl.ds(pl.multiple_of(depth + tile, evo), evo)]
                panel[half + m * evo : half + (m + 1) * evo, lanes] = other_ref[
                    m, pl.ds(pl.multiple_of(tile, evo), evo)
                ]
    for n in range(sub // WIDE):
        rows = slice(n * WIDE, (n + 1) * WIDE)
        added = jnp.zeros((2 * half, WIDE), F32)
        for k in range(chips):
            obs = jnp.concatenate([near_ref[k, rows], far_ref[k, rows]], axis=1)
            added += lax.dot_general(
                panel[:, k * WIDE : (k + 1) * WIDE], obs, NT, preferred_element_type=F32
            )
        s_own[:, :, rows] = added[:half].astype(BF16).reshape(chips, evo, WIDE)
        s_other[:, :, rows] = added[half:].astype(BF16).reshape(chips, evo, WIDE)
        for l in range(WIDE // LANES):
            block = n * (WIDE // LANES) + l
            row = sub + block * 2 * evo
            prior = jnp.concatenate(
                [
                    ref[m, row : row + evo].astype(F32) + ref[m, row + evo : row + 2 * evo].astype(F32)
                    for ref in (near_ref, far_ref)
                    for m in range(chips)
                ],
                axis=0,
            )
            weight = apod_ref[pl.ds(me * (sub // LANES) + block, 1), :]
            value = weight * (prior + added[:, l * LANES : (l + 1) * LANES])
            weighted[:, block * LANES : (block + 1) * LANES] = value.astype(BF16)
    for n in range(prows // WIDE):
        cols = slice(n * WIDE, (n + 1) * WIDE)
        part = lax.dot_general(weighted[...], proj_ref[cols], NT, preferred_element_type=F32)
        p_own[:, :, cols] = part[:half].reshape(chips, evo, WIDE)
        p_other[:, :, cols] = part[half:].reshape(chips, evo, WIDE)


def main_step(me, near, far, other, apod, proj, evo, count):
    chips = near.shape[0]
    prows, sub = proj.shape
    total = 2 * chips * evo
    return pl.pallas_call(
        main_kernel,
        out_shape=(
            jax.ShapeDtypeStruct((chips, evo, prows), F32),
            jax.ShapeDtypeStruct((chips, evo, prows), F32),
            jax.ShapeDtypeStruct((chips, evo, sub), BF16),
            jax.ShapeDtypeStruct((chips, evo, sub), BF16),
        ),
        in_specs=[pl.BlockSpec(memory_space=pltpu.SMEM)] + whole(5),
        out_specs=tuple(whole(4)),
        scratch_shapes=[pltpu.VMEM((total, count), BF16), pltpu.VMEM((total, sub), BF16)],
        compiler_params=pltpu.CompilerParams(vmem_limit_bytes=28 * MIB),
        cost_estimate=cost(2 * total * sub * (count + prows), 4 * near.size + 2 * proj.size + 4 * total * prows),
    )(me, near, far, other, apod, proj)


def home_kernel(p_own, p_got, s_own, s_got, out_ref):
    prows, sub = p_own.shape[2], s_own.shape[2]
    out_ref[:, :, :prows] = (p_own[...] + p_got[...]).astype(BF16)
    out_ref[:, :, prows : prows + sub] = s_own[...]
    out_ref[:, :, prows + sub :] = s_got[...]


def sum_kernel(msg_ref, out_ref):
    width = out_ref.shape[2]
    for n in range(out_ref.shape[0]):
        out_ref[n] = jnp.sum(msg_ref[:, :, n * width : (n + 1) * width].astype(F32), axis=0)


def add_kernel(prows, core_ref, msg_ref, prior_ref, out_ref):
    chips = msg_ref.shape[0]
    sub = prior_ref.shape[1] // (2 * chips)
    core = core_ref[0]
    for m in range(chips):
        for b in range(2):
            at = pl.ds(pl.multiple_of((2 * m + jnp.bitwise_xor(core, b)) * sub, LANES), sub)
            came = msg_ref[m, :, prows + b * sub : prows + (b + 1) * sub].astype(F32)
            out_ref[:, at] = prior_ref[:, at] + came


def swap(x, axis, bits, n):
    return lax.ppermute(x, axis, [(i, i ^ bits) for i in range(n)])


def on_device(n_row, n_col, obs, skies, idx, prior, apod, proj):
    rows_blk, evo = skies.shape
    sub = rows_blk // n_col
    count = idx.shape[0]
    prows = proj.shape[0]
    chips = n_col // 2
    prior_t = prior.T
    me = lax.axis_index("col").astype(jnp.int32)
    first = (lax.axis_index("row") * rows_blk).astype(jnp.int32)
    picked = pick(first.reshape(1), idx.reshape(1, count), skies.T)
    far = swap(picked, "row", n_row // 2, n_row)
    keep, give = pack((me % 2).reshape(1), obs, prior_t, n_col)
    keep, give, far = lax.optimization_barrier((keep, give, far))
    same = [[2 * m + b for m in range(chips)] for b in range(2)]
    to_chips = functools.partial(
        lax.all_to_all, axis_name="col", split_axis=0, concat_axis=0, tiled=True, axis_index_groups=same
    )
    near_rows = to_chips(keep)
    got = swap(give, "col", 1, n_col)
    picked = picked + far
    for group in ((1, 2, 3), (4,)):
        parts = [swap(picked, "row", k, n_row) for k in group]
        for part in parts:
            picked = picked + part
    joined = join(got, picked)
    near_rows, joined = lax.optimization_barrier((near_rows, joined))
    far_rows = to_chips(joined)
    other = swap(far_rows[:, keep.shape[1] :], "col", 1, n_col)

    p_own, p_other, s_own, s_other = main_step(
        me.reshape(1), near_rows, far_rows, other, apod.reshape(rows_blk // LANES, LANES), proj, evo, count
    )
    p_got = swap(p_other, "col", 1, n_col)
    s_got = swap(s_other, "col", 1, n_col)
    home = pl.pallas_call(
        home_kernel,
        out_shape=jax.ShapeDtypeStruct((chips, evo, prows + 2 * sub), BF16),
        in_specs=whole(4),
        out_specs=whole(1)[0],
        compiler_params=pltpu.CompilerParams(vmem_limit_bytes=16 * MIB),
        cost_estimate=cost(p_own.size, 10 * p_own.size),
    )(p_own, p_got, s_own, s_got)
    home = to_chips(home)
    share = pl.pallas_call(
        sum_kernel,
        out_shape=jax.ShapeDtypeStruct((n_row, evo, prows // n_row), F32),
        in_specs=whole(1),
        out_specs=whole(1)[0],
        cost_estimate=cost(home.size, 2 * home.size),
    )(home)
    share = lax.all_to_all(share, "row", 0, 0, tiled=True)
    projection = share.sum(0).T
    reobserved = pl.pallas_call(
        functools.partial(add_kernel, prows),
        out_shape=jax.ShapeDtypeStruct((evo, rows_blk), F32),
        in_specs=[pl.BlockSpec(memory_space=pltpu.SMEM)] + whole(2),
        out_specs=whole(1)[0],
        cost_estimate=cost(prior.size, 10 * prior.size),
    )((me % 2).reshape(1), home, prior_t).T
    return reobserved, projection


def solution(mesh):
    n_row, n_col = mesh.shape["row"], mesh.shape["col"]
    return jax.shard_map(
        functools.partial(on_device, n_row, n_col),
        mesh=mesh,
        in_specs=(P("row", "col"), P("row", "col"), P(), P("row", "col"), P("row"), P(None, ("row", "col"))),
        out_specs=(P("row", "col"), P("row", "col")),
        check_vma=False,
    )
```

```python
import functools

import jax
import jax.numpy as jnp
from jax import lax
from jax.experimental import pallas as pl
from jax.experimental.pallas import tpu as pltpu
from jax.sharding import PartitionSpec as P

F32, BF16 = jnp.float32, jnp.bfloat16
LANES = 128
WIDE = 256
MIB = 1 << 20
NT = (((1,), (1,)), ((), ()))


def whole(n):
    return [pl.BlockSpec(memory_space=pltpu.VMEM)] * n


def cost(flops, nbytes):
    return pl.CostEstimate(flops=flops, bytes_accessed=nbytes, transcendentals=0)


def pack_kernel(chips, core_ref, obs_ref, prior_ref, keep_ref, give_ref):
    sub = obs_ref.shape[0] // (2 * chips)
    evo = prior_ref.shape[0]
    for m in range(chips):
        for side, out_ref in enumerate((keep_ref, give_ref)):
            start = pl.multiple_of((2 * m + jnp.bitwise_xor(core_ref[0], side)) * sub, LANES)
            out_ref[m, :sub] = obs_ref[pl.ds(start, sub)]
            for l in range(sub // LANES):
                value = prior_ref[:, pl.ds(pl.multiple_of(start + l * LANES, LANES), LANES)]
                high = value.astype(BF16)
                row = sub + l * 2 * evo
                out_ref[m, row : row + evo] = high
                out_ref[m, row + evo : row + 2 * evo] = (value - high.astype(F32)).astype(BF16)


def pack(core, obs, prior_t, n_col, spare):
    rows, width = obs.shape
    evo = prior_t.shape[0]
    sub = rows // n_col
    depth = sub + 2 * evo * sub // LANES
    chips = 2
    block = pl.BlockSpec((chips, depth, width), lambda i, _: (i, 0, 0))
    return pl.pallas_call(
        functools.partial(pack_kernel, chips),
        out_shape=[jax.ShapeDtypeStruct((n_col // 2, depth + more, width), BF16) for more in (0, spare)],
        grid_spec=pltpu.PrefetchScalarGridSpec(
            num_scalar_prefetch=1,
            grid=(n_col // 2 // chips,),
            in_specs=[
                pl.BlockSpec((2 * chips * sub, width), lambda i, _: (i, 0)),
                pl.BlockSpec((evo, 2 * chips * sub), lambda i, _: (0, i)),
            ],
            out_specs=[block] * 2,
        ),
        cost_estimate=cost(0, 2 * 2 * n_col * depth * width),
    )(core, obs, prior_t)


def join_kernel(depth, got_ref, picked_ref, out_ref, tiles, sems):
    evo, count = picked_ref.shape
    for l in range(count // LANES):
        tiles[l * evo : (l + 1) * evo] = picked_ref[:, l * LANES : (l + 1) * LANES]
    copies = [
        pltpu.make_async_copy(tiles, out_ref.at[m, pl.ds(depth, tiles.shape[0])], sems.at[m])
        for m in range(out_ref.shape[0])
    ]
    for copy in copies:
        copy.start()
    for copy in copies:
        copy.wait()


def join(got, picked, depth):
    chips, full, width = got.shape
    anywhere = pl.BlockSpec(memory_space=pl.ANY)
    return pl.pallas_call(
        functools.partial(join_kernel, depth),
        out_shape=jax.ShapeDtypeStruct(got.shape, BF16),
        in_specs=[anywhere] + whole(1),
        out_specs=anywhere,
        scratch_shapes=[pltpu.VMEM((full - depth, width), BF16), pltpu.SemaphoreType.DMA((chips,))],
        input_output_aliases={0: 0},
        cost_estimate=cost(0, 2 * chips * (full - depth) * width),
    )(got, picked)


def pick_kernel(first_ref, idx_ref, sky_ref, out_ref):
    evo, rows = sky_ref.shape
    groups = rows // WIDE
    local = idx_ref[...] - first_ref[0]
    place = lax.broadcasted_iota(jnp.int32, (WIDE, local.shape[1]), 0)
    onehot = jnp.where(place == (local & (WIDE - 1)), 1.0, 0.0).astype(BF16)
    group = lax.shift_right_arithmetic(local, WIDE.bit_length() - 1)
    total = jnp.zeros(out_ref.shape, F32)
    step = 16
    for start in range(0, groups, step):
        block = jnp.concatenate(
            [sky_ref[:, g * WIDE : (g + 1) * WIDE] for g in range(start, start + step)], axis=0
        )
        found = jnp.dot(block, onehot, preferred_element_type=F32)
        for g in range(step):
            total = total + jnp.where(group == start + g, found[g * evo : (g + 1) * evo], 0.0)
    out_ref[...] = total.astype(BF16)


def pick(first, idx, sky):
    evo, rows = sky.shape
    count = idx.shape[1]
    tile = 512
    return pl.pallas_call(
        pick_kernel,
        out_shape=jax.ShapeDtypeStruct((evo, count), BF16),
        grid_spec=pltpu.PrefetchScalarGridSpec(
            num_scalar_prefetch=1,
            grid=(count // tile,),
            in_specs=[
                pl.BlockSpec((1, tile), lambda i, _: (0, i)),
                pl.BlockSpec((evo, rows), lambda i, _: (0, 0)),
            ],
            out_specs=pl.BlockSpec((evo, tile), lambda i, _: (0, i)),
        ),
        cost_estimate=cost(2 * evo * rows * count, 2 * evo * rows + 2 * evo * count),
    )(first, idx, sky)


def main_kernel(
    me_ref, near_ref, far_ref, other_ref, apod_ref, proj_ref, p_own, p_other, s_own, s_other, panel, weighted
):
    chips, evo, _ = p_own.shape
    prows, sub = proj_ref.shape
    me = me_ref[0]
    core = me % 2
    half = chips * evo
    depth = near_ref.shape[1]
    for k in range(chips):
        for side in range(2):
            tile = (2 * k + jnp.bitwise_xor(core, side)) * evo
            lanes = slice((2 * k + side) * LANES, (2 * k + side + 1) * LANES)
            for m in range(chips):
                panel[m * evo : (m + 1) * evo, lanes] = far_ref[m, pl.ds(pl.multiple_of(depth + tile, evo), evo)]
                panel[half + m * evo : half + (m + 1) * evo, lanes] = other_ref[
                    m, pl.ds(pl.multiple_of(tile, evo), evo)
                ]
    for n in range(sub // WIDE):
        rows = slice(n * WIDE, (n + 1) * WIDE)
        added = jnp.zeros((2 * half, WIDE), F32)
        for k in range(chips):
            obs = jnp.concatenate([near_ref[k, rows], far_ref[k, rows]], axis=1)
            added += lax.dot_general(
                panel[:, k * WIDE : (k + 1) * WIDE], obs, NT, preferred_element_type=F32
            )
        s_own[:, :, rows] = added[:half].astype(BF16).reshape(chips, evo, WIDE)
        s_other[:, :, rows] = added[half:].astype(BF16).reshape(chips, evo, WIDE)
        for l in range(WIDE // LANES):
            block = n * (WIDE // LANES) + l
            row = sub + block * 2 * evo
            prior = jnp.concatenate(
                [
                    ref[m, row : row + evo].astype(F32) + ref[m, row + evo : row + 2 * evo].astype(F32)
                    for ref in (near_ref, far_ref)
                    for m in range(chips)
                ],
                axis=0,
            )
            weight = apod_ref[pl.ds(me * (sub // LANES) + block, 1), :]
            value = weight * (prior + added[:, l * LANES : (l + 1) * LANES])
            weighted[:, block * LANES : (block + 1) * LANES] = value.astype(BF16)
    for n in range(prows // WIDE):
        cols = slice(n * WIDE, (n + 1) * WIDE)
        part = lax.dot_general(weighted[...], proj_ref[cols], NT, preferred_element_type=F32)
        p_own[:, :, cols] = part[:half].reshape(chips, evo, WIDE)
        p_other[:, :, cols] = part[half:].reshape(chips, evo, WIDE)


def main_step(me, near, far, other, apod, proj, evo, count):
    chips = near.shape[0]
    prows, sub = proj.shape
    total = 2 * chips * evo
    return pl.pallas_call(
        main_kernel,
        out_shape=(
            jax.ShapeDtypeStruct((chips, evo, prows), F32),
            jax.ShapeDtypeStruct((chips, evo, prows), F32),
            jax.ShapeDtypeStruct((chips, evo, sub), BF16),
            jax.ShapeDtypeStruct((chips, evo, sub), BF16),
        ),
        in_specs=[pl.BlockSpec(memory_space=pltpu.SMEM)] + whole(5),
        out_specs=tuple(whole(4)),
        scratch_shapes=[pltpu.VMEM((total, count), BF16), pltpu.VMEM((total, sub), BF16)],
        compiler_params=pltpu.CompilerParams(vmem_limit_bytes=28 * MIB),
        cost_estimate=cost(2 * total * sub * (count + prows), 4 * near.size + 2 * proj.size + 4 * total * prows),
    )(me, near, far, other, apod, proj)


def home_kernel(p_own, p_got, s_own, s_got, out_ref):
    prows, sub = p_own.shape[2], s_own.shape[2]
    out_ref[:, :, :prows] = (p_own[...] + p_got[...]).astype(BF16)
    out_ref[:, :, prows : prows + sub] = s_own[...]
    out_ref[:, :, prows + sub :] = s_got[...]


def sum_kernel(msg_ref, out_ref):
    width = out_ref.shape[2]
    for n in range(out_ref.shape[0]):
        out_ref[n] = jnp.sum(msg_ref[:, :, n * width : (n + 1) * width].astype(F32), axis=0)


def add_kernel(prows, core_ref, msg_ref, prior_ref, out_ref):
    chips = msg_ref.shape[0]
    sub = prior_ref.shape[1] // (2 * chips)
    core = core_ref[0]
    for m in range(chips):
        for b in range(2):
            at = pl.ds(pl.multiple_of((2 * m + jnp.bitwise_xor(core, b)) * sub, LANES), sub)
            came = msg_ref[m, :, prows + b * sub : prows + (b + 1) * sub].astype(F32)
            out_ref[:, at] = prior_ref[:, at] + came


def add_up(x, n_row):
    ring = n_row // 2

    def turn(y, by):
        return lax.ppermute(
            y, "row", [(h * ring + z, h * ring + (z + by) % ring) for h in range(2) for z in range(ring)]
        )

    below, above = turn(x, 1), turn(x, -1)
    two = x + above
    three = two + below
    x = three + turn(three, -3) + turn(two, 3)
    return x + swap(x, "row", ring, n_row)


def swap(x, axis, bits, n):
    return lax.ppermute(x, axis, [(i, i ^ bits) for i in range(n)])


def on_device(n_row, n_col, obs, skies, idx, prior, apod, proj):
    rows_blk, evo = skies.shape
    sub = rows_blk // n_col
    count = idx.shape[0]
    prows = proj.shape[0]
    chips = n_col // 2
    prior_t = prior.T
    me = lax.axis_index("col").astype(jnp.int32)
    core = (me % 2).reshape(1)
    first = (lax.axis_index("row") * rows_blk).astype(jnp.int32)
    same = [[2 * m + b for m in range(chips)] for b in range(2)]
    to_chips = functools.partial(
        lax.all_to_all, axis_name="col", split_axis=0, concat_axis=0, tiled=True, axis_index_groups=same
    )
    keep, give = pack(core, obs, prior_t, n_col, count * evo // LANES)
    keep, give, idx = lax.optimization_barrier((keep, give, idx))
    near_rows = to_chips(keep)
    picked = pick(first.reshape(1), idx.reshape(1, count), skies.T)
    got = swap(give, "col", 1, n_col)
    picked = add_up(picked, n_row)
    joined = join(got, picked, keep.shape[1])
    near_rows, joined = lax.optimization_barrier((near_rows, joined))
    far_rows = to_chips(joined)
    other = swap(far_rows[:, keep.shape[1] :], "col", 1, n_col)

    p_own, p_other, s_own, s_other = main_step(
        me.reshape(1), near_rows, far_rows, other, apod.reshape(rows_blk // LANES, LANES), proj, evo, count
    )
    p_got = swap(p_other, "col", 1, n_col)
    s_got = swap(s_other, "col", 1, n_col)
    home = pl.pallas_call(
        home_kernel,
        out_shape=jax.ShapeDtypeStruct((chips, evo, prows + 2 * sub), BF16),
        in_specs=whole(4),
        out_specs=whole(1)[0],
        compiler_params=pltpu.CompilerParams(vmem_limit_bytes=16 * MIB),
        cost_estimate=cost(p_own.size, 10 * p_own.size),
    )(p_own, p_got, s_own, s_got)
    home = to_chips(home)
    share = pl.pallas_call(
        sum_kernel,
        out_shape=jax.ShapeDtypeStruct((n_row, evo, prows // n_row), F32),
        grid=(1,),
        in_specs=[pl.BlockSpec((chips, evo, prows), lambda i: (0, 0, 0))],
        out_specs=pl.BlockSpec((n_row, evo, prows // n_row), lambda i: (0, 0, 0)),
        cost_estimate=cost(home.size, 2 * home.size),
    )(home)
    share = lax.all_to_all(share, "row", 0, 0, tiled=True)
    projection = share.sum(0).T
    reobserved = pl.pallas_call(
        functools.partial(add_kernel, prows),
        out_shape=jax.ShapeDtypeStruct((evo, rows_blk), F32),
        in_specs=[pl.BlockSpec(memory_space=pltpu.SMEM)] + whole(2),
        out_specs=whole(1)[0],
        cost_estimate=cost(prior.size, 10 * prior.size),
    )(core, home, prior_t).T
    return reobserved, projection


def solution(mesh):
    n_row, n_col = mesh.shape["row"], mesh.shape["col"]
    return jax.shard_map(
        functools.partial(on_device, n_row, n_col),
        mesh=mesh,
        in_specs=(P("row", "col"), P("row", "col"), P(), P("row", "col"), P("row"), P(None, ("row", "col"))),
        out_specs=(P("row", "col"), P("row", "col")),
        check_vma=False,
    )
```

```python
import functools

import jax
import jax.numpy as jnp
from jax import lax
from jax.experimental import pallas as pl
from jax.experimental.pallas import tpu as pltpu
from jax.sharding import PartitionSpec as P

F32, BF16 = jnp.float32, jnp.bfloat16
LANES = 128
WIDE = 256
MIB = 1 << 20
NT = (((1,), (1,)), ((), ()))


def whole(n):
    return [pl.BlockSpec(memory_space=pltpu.VMEM)] * n


def cost(flops, nbytes):
    return pl.CostEstimate(flops=flops, bytes_accessed=nbytes, transcendentals=0)


def pack_kernel(chips, core_ref, obs_ref, prior_ref, keep_ref, give_ref):
    sub = obs_ref.shape[0] // (2 * chips)
    evo = prior_ref.shape[0]
    for m in range(chips):
        for side, out_ref in enumerate((keep_ref, give_ref)):
            start = pl.multiple_of((2 * m + jnp.bitwise_xor(core_ref[0], side)) * sub, LANES)
            out_ref[m, :sub] = obs_ref[pl.ds(start, sub)]
            for l in range(sub // LANES):
                value = prior_ref[:, pl.ds(pl.multiple_of(start + l * LANES, LANES), LANES)]
                high = value.astype(BF16)
                row = sub + l * 2 * evo
                out_ref[m, row : row + evo] = high
                out_ref[m, row + evo : row + 2 * evo] = (value - high.astype(F32)).astype(BF16)


def pack(core, obs, prior_t, n_col, spare):
    rows, width = obs.shape
    evo = prior_t.shape[0]
    sub = rows // n_col
    depth = sub + 2 * evo * sub // LANES
    chips = 4
    block = pl.BlockSpec((chips, depth, width), lambda i, _: (i, 0, 0))
    return pl.pallas_call(
        functools.partial(pack_kernel, chips),
        out_shape=[jax.ShapeDtypeStruct((n_col // 2, depth + more, width), BF16) for more in (0, spare)],
        grid_spec=pltpu.PrefetchScalarGridSpec(
            num_scalar_prefetch=1,
            grid=(n_col // 2 // chips,),
            in_specs=[
                pl.BlockSpec((2 * chips * sub, width), lambda i, _: (i, 0)),
                pl.BlockSpec((evo, 2 * chips * sub), lambda i, _: (0, i)),
            ],
            out_specs=[block] * 2,
        ),
        cost_estimate=cost(0, 2 * 2 * n_col * depth * width),
    )(core, obs, prior_t)


def join_kernel(depth, got_ref, picked_ref, out_ref, tiles, sems):
    evo, count = picked_ref.shape
    for l in range(count // LANES):
        tiles[l * evo : (l + 1) * evo] = picked_ref[:, l * LANES : (l + 1) * LANES]
    copies = [
        pltpu.make_async_copy(tiles, out_ref.at[m, pl.ds(depth, tiles.shape[0])], sems.at[m])
        for m in range(out_ref.shape[0])
    ]
    for copy in copies:
        copy.start()
    for copy in copies:
        copy.wait()


def join(got, picked, depth):
    chips, full, width = got.shape
    anywhere = pl.BlockSpec(memory_space=pl.ANY)
    return pl.pallas_call(
        functools.partial(join_kernel, depth),
        out_shape=jax.ShapeDtypeStruct(got.shape, BF16),
        in_specs=[anywhere] + whole(1),
        out_specs=anywhere,
        scratch_shapes=[pltpu.VMEM((full - depth, width), BF16), pltpu.SemaphoreType.DMA((chips,))],
        input_output_aliases={0: 0},
        cost_estimate=cost(0, 2 * chips * (full - depth) * width),
    )(got, picked)


def pick_kernel(first_ref, idx_ref, sky_ref, out_ref):
    evo, rows = sky_ref.shape
    groups = rows // WIDE
    local = idx_ref[...] - first_ref[0]
    place = lax.broadcasted_iota(jnp.int32, (WIDE, local.shape[1]), 0)
    onehot = jnp.where(place == (local & (WIDE - 1)), 1.0, 0.0).astype(BF16)
    group = lax.shift_right_arithmetic(local, WIDE.bit_length() - 1)
    total = jnp.zeros(out_ref.shape, F32)
    step = 16
    for start in range(0, groups, step):
        block = jnp.concatenate(
            [sky_ref[:, g * WIDE : (g + 1) * WIDE] for g in range(start, start + step)], axis=0
        )
        found = jnp.dot(block, onehot, preferred_element_type=F32)
        for g in range(step):
            total = total + jnp.where(group == start + g, found[g * evo : (g + 1) * evo], 0.0)
    out_ref[...] = total.astype(BF16)


def pick(first, idx, sky):
    evo, rows = sky.shape
    count = idx.shape[1]
    tile = 1024
    return pl.pallas_call(
        pick_kernel,
        out_shape=jax.ShapeDtypeStruct((evo, count), BF16),
        grid_spec=pltpu.PrefetchScalarGridSpec(
            num_scalar_prefetch=1,
            grid=(count // tile,),
            in_specs=[
                pl.BlockSpec((1, tile), lambda i, _: (0, i)),
                pl.BlockSpec((evo, rows), lambda i, _: (0, 0)),
            ],
            out_specs=pl.BlockSpec((evo, tile), lambda i, _: (0, i)),
        ),
        cost_estimate=cost(2 * evo * rows * count, 2 * evo * rows + 2 * evo * count),
    )(first, idx, sky)


def main_kernel(
    me_ref, near_ref, far_ref, other_ref, apod_ref, proj_ref, p_own, p_other, s_own, s_other, panel, weighted
):
    chips, evo, _ = p_own.shape
    prows, sub = proj_ref.shape
    me = me_ref[0]
    core = me % 2
    half = chips * evo
    depth = near_ref.shape[1]
    for k in range(chips):
        for side in range(2):
            tile = (2 * k + jnp.bitwise_xor(core, side)) * evo
            lanes = slice((2 * k + side) * LANES, (2 * k + side + 1) * LANES)
            for m in range(chips):
                panel[m * evo : (m + 1) * evo, lanes] = far_ref[m, pl.ds(pl.multiple_of(depth + tile, evo), evo)]
                panel[half + m * evo : half + (m + 1) * evo, lanes] = other_ref[
                    m, pl.ds(pl.multiple_of(tile, evo), evo)
                ]
    for n in range(sub // WIDE):
        rows = slice(n * WIDE, (n + 1) * WIDE)
        added = jnp.zeros((2 * half, WIDE), F32)
        for k in range(chips):
            obs = jnp.concatenate([near_ref[k, rows], far_ref[k, rows]], axis=1)
            added += lax.dot_general(
                panel[:, k * WIDE : (k + 1) * WIDE], obs, NT, preferred_element_type=F32
            )
        s_own[:, :, rows] = added[:half].astype(BF16).reshape(chips, evo, WIDE)
        s_other[:, :, rows] = added[half:].astype(BF16).reshape(chips, evo, WIDE)
        for l in range(WIDE // LANES):
            block = n * (WIDE // LANES) + l
            row = sub + block * 2 * evo
            prior = jnp.concatenate(
                [
                    ref[m, row : row + evo].astype(F32) + ref[m, row + evo : row + 2 * evo].astype(F32)
                    for ref in (near_ref, far_ref)
                    for m in range(chips)
                ],
                axis=0,
            )
            weight = apod_ref[pl.ds(me * (sub // LANES) + block, 1), :]
            value = weight * (prior + added[:, l * LANES : (l + 1) * LANES])
            weighted[:, block * LANES : (block + 1) * LANES] = value.astype(BF16)
    for n in range(prows // WIDE):
        cols = slice(n * WIDE, (n + 1) * WIDE)
        part = lax.dot_general(weighted[...], proj_ref[cols], NT, preferred_element_type=F32)
        p_own[:, :, cols] = part[:half].reshape(chips, evo, WIDE)
        p_other[:, :, cols] = part[half:].reshape(chips, evo, WIDE)


def main_step(me, near, far, other, apod, proj, evo, count):
    chips = near.shape[0]
    prows, sub = proj.shape
    total = 2 * chips * evo
    return pl.pallas_call(
        main_kernel,
        out_shape=(
            jax.ShapeDtypeStruct((chips, evo, prows), F32),
            jax.ShapeDtypeStruct((chips, evo, prows), F32),
            jax.ShapeDtypeStruct((chips, evo, sub), BF16),
            jax.ShapeDtypeStruct((chips, evo, sub), BF16),
        ),
        in_specs=[pl.BlockSpec(memory_space=pltpu.SMEM)] + whole(5),
        out_specs=tuple(whole(4)),
        scratch_shapes=[pltpu.VMEM((total, count), BF16), pltpu.VMEM((total, sub), BF16)],
        compiler_params=pltpu.CompilerParams(vmem_limit_bytes=28 * MIB),
        cost_estimate=cost(2 * total * sub * (count + prows), 4 * near.size + 2 * proj.size + 4 * total * prows),
    )(me, near, far, other, apod, proj)


def home_kernel(p_own, p_got, s_own, s_got, out_ref):
    prows, sub = p_own.shape[2], s_own.shape[2]
    out_ref[:, :, :prows] = (p_own[...] + p_got[...]).astype(BF16)
    out_ref[:, :, prows : prows + sub] = s_own[...]
    out_ref[:, :, prows + sub :] = s_got[...]


def sum_kernel(msg_ref, out_ref):
    width = out_ref.shape[2]
    for n in range(out_ref.shape[0]):
        out_ref[n] = jnp.sum(msg_ref[:, :, n * width : (n + 1) * width].astype(F32), axis=0)


def add_kernel(prows, core_ref, msg_ref, prior_ref, out_ref):
    chips = msg_ref.shape[0]
    sub = prior_ref.shape[1] // (2 * chips)
    core = core_ref[0]
    for m in range(chips):
        for b in range(2):
            at = pl.ds(pl.multiple_of((2 * m + jnp.bitwise_xor(core, b)) * sub, LANES), sub)
            came = msg_ref[m, :, prows + b * sub : prows + (b + 1) * sub].astype(F32)
            out_ref[:, at] = prior_ref[:, at] + came


def add_up(x, n_row):
    ring = n_row // 2

    def turn(y, by):
        return lax.ppermute(
            y, "row", [(h * ring + z, h * ring + (z + by) % ring) for h in range(2) for z in range(ring)]
        )

    below, above = turn(x, 1), turn(x, -1)
    two = x + above
    three = two + below
    x = three + turn(three, -3) + turn(two, 3)
    return x + swap(x, "row", ring, n_row)


def swap(x, axis, bits, n):
    return lax.ppermute(x, axis, [(i, i ^ bits) for i in range(n)])


def on_device(n_row, n_col, obs, skies, idx, prior, apod, proj):
    rows_blk, evo = skies.shape
    sub = rows_blk // n_col
    count = idx.shape[0]
    prows = proj.shape[0]
    chips = n_col // 2
    prior_t = prior.T
    me = lax.axis_index("col").astype(jnp.int32)
    core = (me % 2).reshape(1)
    first = (lax.axis_index("row") * rows_blk).astype(jnp.int32)
    same = [[2 * m + b for m in range(chips)] for b in range(2)]
    to_chips = functools.partial(
        lax.all_to_all, axis_name="col", split_axis=0, concat_axis=0, tiled=True, axis_index_groups=same
    )
    keep, give = pack(core, obs, prior_t, n_col, count * evo // LANES)
    keep, give, idx = lax.optimization_barrier((keep, give, idx))
    near_rows = to_chips(keep)
    picked = pick(first.reshape(1), idx.reshape(1, count), skies.T)
    got = swap(give, "col", 1, n_col)
    picked = add_up(picked, n_row)
    joined = join(got, picked, keep.shape[1])
    near_rows, joined = lax.optimization_barrier((near_rows, joined))
    far_rows = to_chips(joined)
    other = swap(far_rows[:, keep.shape[1] :], "col", 1, n_col)

    p_own, p_other, s_own, s_other = main_step(
        me.reshape(1), near_rows, far_rows, other, apod.reshape(rows_blk // LANES, LANES), proj, evo, count
    )
    p_got = swap(p_other, "col", 1, n_col)
    s_got = swap(s_other, "col", 1, n_col)
    home = pl.pallas_call(
        home_kernel,
        out_shape=jax.ShapeDtypeStruct((chips, evo, prows + 2 * sub), BF16),
        in_specs=whole(4),
        out_specs=whole(1)[0],
        compiler_params=pltpu.CompilerParams(vmem_limit_bytes=16 * MIB),
        cost_estimate=cost(p_own.size, 10 * p_own.size),
    )(p_own, p_got, s_own, s_got)
    home = to_chips(home)
    share = pl.pallas_call(
        sum_kernel,
        out_shape=jax.ShapeDtypeStruct((n_row, evo, prows // n_row), F32),
        grid=(1,),
        in_specs=[pl.BlockSpec((chips, evo, prows), lambda i: (0, 0, 0))],
        out_specs=pl.BlockSpec((n_row, evo, prows // n_row), lambda i: (0, 0, 0)),
        cost_estimate=cost(home.size, 2 * home.size),
    )(home)
    share = lax.all_to_all(share, "row", 0, 0, tiled=True)
    projection = share.sum(0).T
    reobserved = pl.pallas_call(
        functools.partial(add_kernel, prows),
        out_shape=jax.ShapeDtypeStruct((evo, rows_blk), F32),
        in_specs=[pl.BlockSpec(memory_space=pltpu.SMEM)] + whole(2),
        out_specs=whole(1)[0],
        cost_estimate=cost(prior.size, 10 * prior.size),
    )(core, home, prior_t).T
    return reobserved, projection


def solution(mesh):
    n_row, n_col = mesh.shape["row"], mesh.shape["col"]
    return jax.shard_map(
        functools.partial(on_device, n_row, n_col),
        mesh=mesh,
        in_specs=(P("row", "col"), P("row", "col"), P(), P("row", "col"), P("row"), P(None, ("row", "col"))),
        out_specs=(P("row", "col"), P("row", "col")),
        check_vma=False,
    )
```

```python
import functools

import jax
import jax.numpy as jnp
from jax import lax
from jax.experimental import pallas as pl
from jax.experimental.pallas import tpu as pltpu
from jax.sharding import PartitionSpec as P

F32, BF16 = jnp.float32, jnp.bfloat16
LANES = 128
WIDE = 256
MIB = 1 << 20
NT = (((1,), (1,)), ((), ()))


def whole(n):
    return [pl.BlockSpec(memory_space=pltpu.VMEM)] * n


def cost(flops, nbytes):
    return pl.CostEstimate(flops=flops, bytes_accessed=nbytes, transcendentals=0)


def pack_kernel(chips, core_ref, obs_ref, prior_ref, keep_ref, give_ref):
    sub = obs_ref.shape[0] // (2 * chips)
    evo = prior_ref.shape[0]
    for m in range(chips):
        for side, out_ref in enumerate((keep_ref, give_ref)):
            start = pl.multiple_of((2 * m + jnp.bitwise_xor(core_ref[0], side)) * sub, LANES)
            out_ref[m, :sub] = obs_ref[pl.ds(start, sub)]
            for l in range(sub // LANES):
                value = prior_ref[:, pl.ds(pl.multiple_of(start + l * LANES, LANES), LANES)]
                high = value.astype(BF16)
                row = sub + l * 2 * evo
                out_ref[m, row : row + evo] = high
                out_ref[m, row + evo : row + 2 * evo] = (value - high.astype(F32)).astype(BF16)


def pack(core, obs, prior_t, n_col, spare):
    rows, width = obs.shape
    evo = prior_t.shape[0]
    sub = rows // n_col
    depth = sub + 2 * evo * sub // LANES
    chips = 4
    block = pl.BlockSpec((chips, depth, width), lambda i, _: (i, 0, 0))
    return pl.pallas_call(
        functools.partial(pack_kernel, chips),
        out_shape=[jax.ShapeDtypeStruct((n_col // 2, depth + more, width), BF16) for more in (0, spare)],
        grid_spec=pltpu.PrefetchScalarGridSpec(
            num_scalar_prefetch=1,
            grid=(n_col // 2 // chips,),
            in_specs=[
                pl.BlockSpec((2 * chips * sub, width), lambda i, _: (i, 0)),
                pl.BlockSpec((evo, 2 * chips * sub), lambda i, _: (0, i)),
            ],
            out_specs=[block] * 2,
        ),
        cost_estimate=cost(0, 2 * 2 * n_col * depth * width),
    )(core, obs, prior_t)


def join_kernel(depth, got_ref, picked_ref, out_ref, tiles, sems):
    evo, count = picked_ref.shape
    for l in range(count // LANES):
        tiles[l * evo : (l + 1) * evo] = picked_ref[:, l * LANES : (l + 1) * LANES]
    copies = [
        pltpu.make_async_copy(tiles, out_ref.at[m, pl.ds(depth, tiles.shape[0])], sems.at[m])
        for m in range(out_ref.shape[0])
    ]
    for copy in copies:
        copy.start()
    for copy in copies:
        copy.wait()


def join(got, picked, depth):
    chips, full, width = got.shape
    anywhere = pl.BlockSpec(memory_space=pl.ANY)
    return pl.pallas_call(
        functools.partial(join_kernel, depth),
        out_shape=jax.ShapeDtypeStruct(got.shape, BF16),
        in_specs=[anywhere] + whole(1),
        out_specs=anywhere,
        scratch_shapes=[pltpu.VMEM((full - depth, width), BF16), pltpu.SemaphoreType.DMA((chips,))],
        input_output_aliases={0: 0},
        cost_estimate=cost(0, 2 * chips * (full - depth) * width),
    )(got, picked)


def pick_kernel(first_ref, idx_ref, sky_ref, out_ref):
    evo, rows = sky_ref.shape
    groups = rows // WIDE
    local = idx_ref[...] - first_ref[0]
    place = lax.broadcasted_iota(jnp.int32, (WIDE, local.shape[1]), 0)
    onehot = jnp.where(place == (local & (WIDE - 1)), 1.0, 0.0).astype(BF16)
    group = lax.shift_right_arithmetic(local, WIDE.bit_length() - 1)
    total = jnp.zeros(out_ref.shape, F32)
    step = 16
    for start in range(0, groups, step):
        block = jnp.concatenate(
            [sky_ref[:, g * WIDE : (g + 1) * WIDE] for g in range(start, start + step)], axis=0
        )
        found = jnp.dot(block, onehot, preferred_element_type=F32)
        for g in range(step):
            total = total + jnp.where(group == start + g, found[g * evo : (g + 1) * evo], 0.0)
    out_ref[...] = total.astype(BF16)


def pick(first, idx, sky):
    evo, rows = sky.shape
    count = idx.shape[1]
    tile = 1024
    return pl.pallas_call(
        pick_kernel,
        out_shape=jax.ShapeDtypeStruct((evo, count), BF16),
        grid_spec=pltpu.PrefetchScalarGridSpec(
            num_scalar_prefetch=1,
            grid=(count // tile,),
            in_specs=[
                pl.BlockSpec((1, tile), lambda i, _: (0, i)),
                pl.BlockSpec((evo, rows), lambda i, _: (0, 0)),
            ],
            out_specs=pl.BlockSpec((evo, tile), lambda i, _: (0, i)),
        ),
        cost_estimate=cost(2 * evo * rows * count, 2 * evo * rows + 2 * evo * count),
    )(first, idx, sky)


def main_kernel(
    at_pick, me_ref, near_ref, far_ref, pick_ref, prior_ref, apod_ref, proj_ref, p_ref, s_ref, panel, weighted
):
    chips, evo, _ = p_ref.shape
    prows, sub = proj_ref.shape
    me = me_ref[0]
    core = me % 2
    half = chips * evo
    for k in range(chips):
        for side in range(2):
            tile = pl.ds(pl.multiple_of(at_pick + (2 * k + jnp.bitwise_xor(core, side)) * evo, evo), evo)
            lanes = slice((2 * k + side) * LANES, (2 * k + side + 1) * LANES)
            for m in range(chips):
                panel[m * evo : (m + 1) * evo, lanes] = pick_ref[m, tile]
    for n in range(sub // WIDE):
        rows = slice(n * WIDE, (n + 1) * WIDE)
        added = jnp.zeros((half, WIDE), F32)
        for k in range(chips):
            obs = jnp.concatenate([near_ref[k, rows], far_ref[k, rows]], axis=1)
            added += lax.dot_general(
                panel[:, k * WIDE : (k + 1) * WIDE], obs, NT, preferred_element_type=F32
            )
        s_ref[:, :, rows] = added.astype(BF16).reshape(chips, evo, WIDE)
        for l in range(WIDE // LANES):
            block = n * (WIDE // LANES) + l
            row = sub + block * 2 * evo
            prior = jnp.concatenate(
                [
                    prior_ref[m, row : row + evo].astype(F32) + prior_ref[m, row + evo : row + 2 * evo].astype(F32)
                    for m in range(chips)
                ],
                axis=0,
            )
            weight = apod_ref[pl.ds(me * (sub // LANES) + block, 1), :]
            value = weight * (prior + added[:, l * LANES : (l + 1) * LANES])
            weighted[:, block * LANES : (block + 1) * LANES] = value.astype(BF16)
    for n in range(prows // WIDE):
        cols = slice(n * WIDE, (n + 1) * WIDE)
        part = lax.dot_general(weighted[...], proj_ref[cols], NT, preferred_element_type=F32)
        p_ref[:, :, cols] = part.reshape(chips, evo, WIDE)


def main_step(at_pick, me, near, far, picks, prior, apod, proj, evo, count):
    chips = near.shape[0]
    prows, sub = proj.shape
    total = chips * evo
    return pl.pallas_call(
        functools.partial(main_kernel, at_pick),
        out_shape=(
            jax.ShapeDtypeStruct((chips, evo, prows), F32),
            jax.ShapeDtypeStruct((chips, evo, sub), BF16),
        ),
        in_specs=[pl.BlockSpec(memory_space=pltpu.SMEM)] + whole(6),
        out_specs=tuple(whole(2)),
        scratch_shapes=[pltpu.VMEM((total, count), BF16), pltpu.VMEM((total, sub), BF16)],
        compiler_params=pltpu.CompilerParams(vmem_limit_bytes=28 * MIB),
        cost_estimate=cost(2 * total * sub * (count + prows), 4 * near.size + 2 * proj.size + 4 * total * prows),
    )(me, near, far, picks, prior, apod, proj)


def home_kernel(p_own, p_got, s_own, s_got, out_ref):
    prows, sub = p_own.shape[2], s_own.shape[2]
    out_ref[:, :, :prows] = (p_own[...] + p_got[...]).astype(BF16)
    out_ref[:, :, prows : prows + sub] = s_own[...]
    out_ref[:, :, prows + sub :] = s_got[...]


def sum_kernel(msg_ref, out_ref):
    width = out_ref.shape[2]
    for n in range(out_ref.shape[0]):
        out_ref[n] = jnp.sum(msg_ref[:, :, n * width : (n + 1) * width].astype(F32), axis=0)


def add_kernel(prows, core_ref, msg_ref, prior_ref, out_ref):
    chips = msg_ref.shape[0]
    sub = prior_ref.shape[1] // (2 * chips)
    core = core_ref[0]
    for m in range(chips):
        for b in range(2):
            at = pl.ds(pl.multiple_of((2 * m + jnp.bitwise_xor(core, b)) * sub, LANES), sub)
            came = msg_ref[m, :, prows + b * sub : prows + (b + 1) * sub].astype(F32)
            out_ref[:, at] = prior_ref[:, at] + came


def add_up(x, n_row):
    ring = n_row // 2

    def turn(y, by):
        return lax.ppermute(
            y, "row", [(h * ring + z, h * ring + (z + by) % ring) for h in range(2) for z in range(ring)]
        )

    below, above = turn(x, 1), turn(x, -1)
    two = x + above
    three = two + below
    x = three + turn(three, -3) + turn(two, 3)
    return x + swap(x, "row", ring, n_row)


def swap(x, axis, bits, n):
    return lax.ppermute(x, axis, [(i, i ^ bits) for i in range(n)])


def on_device(n_row, n_col, obs, skies, idx, prior, apod, proj):
    rows_blk, evo = skies.shape
    sub = rows_blk // n_col
    count = idx.shape[0]
    prows = proj.shape[0]
    chips = n_col // 2
    prior_t = prior.T
    me = lax.axis_index("col").astype(jnp.int32)
    core = (me % 2).reshape(1)
    first = (lax.axis_index("row") * rows_blk).astype(jnp.int32)
    same = [[2 * m + b for m in range(chips)] for b in range(2)]
    to_chips = functools.partial(
        lax.all_to_all, axis_name="col", split_axis=0, concat_axis=0, tiled=True, axis_index_groups=same
    )
    keep, give = pack(core, obs, prior_t, n_col, count * evo // LANES)
    keep, give, idx = lax.optimization_barrier((keep, give, idx))
    near_rows = to_chips(keep)
    picked = pick(first.reshape(1), idx.reshape(1, count), skies.T)
    got = swap(give, "col", 1, n_col)
    picked = add_up(picked, n_row)
    joined = join(got, picked, keep.shape[1])
    near_rows, joined = lax.optimization_barrier((near_rows, joined))
    far_rows = to_chips(joined)
    other = swap(far_rows[:, keep.shape[1] :], "col", 1, n_col)

    weights = apod.reshape(rows_blk // LANES, LANES)
    rest = (weights, proj, evo, count)
    p_own, s_own = main_step(keep.shape[1], me.reshape(1), near_rows, far_rows, far_rows, near_rows, *rest)
    p_other, s_other = main_step(0, me.reshape(1), near_rows, far_rows, other, far_rows, *rest)
    p_got = swap(p_other, "col", 1, n_col)
    s_got = swap(s_other, "col", 1, n_col)
    home = pl.pallas_call(
        home_kernel,
        out_shape=jax.ShapeDtypeStruct((chips, evo, prows + 2 * sub), BF16),
        in_specs=whole(4),
        out_specs=whole(1)[0],
        compiler_params=pltpu.CompilerParams(vmem_limit_bytes=16 * MIB),
        cost_estimate=cost(p_own.size, 10 * p_own.size),
    )(p_own, p_got, s_own, s_got)
    home = to_chips(home)
    share = pl.pallas_call(
        sum_kernel,
        out_shape=jax.ShapeDtypeStruct((n_row, evo, prows // n_row), F32),
        grid=(1,),
        in_specs=[pl.BlockSpec((chips, evo, prows), lambda i: (0, 0, 0))],
        out_specs=pl.BlockSpec((n_row, evo, prows // n_row), lambda i: (0, 0, 0)),
        cost_estimate=cost(home.size, 2 * home.size),
    )(home)
    share = lax.all_to_all(share, "row", 0, 0, tiled=True)
    projection = share.sum(0).T
    reobserved = pl.pallas_call(
        functools.partial(add_kernel, prows),
        out_shape=jax.ShapeDtypeStruct((evo, rows_blk), F32),
        in_specs=[pl.BlockSpec(memory_space=pltpu.SMEM)] + whole(2),
        out_specs=whole(1)[0],
        cost_estimate=cost(prior.size, 10 * prior.size),
    )(core, home, prior_t).T
    return reobserved, projection


def solution(mesh):
    n_row, n_col = mesh.shape["row"], mesh.shape["col"]
    return jax.shard_map(
        functools.partial(on_device, n_row, n_col),
        mesh=mesh,
        in_specs=(P("row", "col"), P("row", "col"), P(), P("row", "col"), P("row"), P(None, ("row", "col"))),
        out_specs=(P("row", "col"), P("row", "col")),
        check_vma=False,
    )
```

```python
import functools

import jax
import jax.numpy as jnp
from jax import lax
from jax.experimental import pallas as pl
from jax.experimental.pallas import tpu as pltpu
from jax.sharding import PartitionSpec as P

F32, BF16 = jnp.float32, jnp.bfloat16
LANES = 128
WIDE = 256
MIB = 1 << 20
NT = (((1,), (1,)), ((), ()))


def whole(n):
    return [pl.BlockSpec(memory_space=pltpu.VMEM)] * n


def cost(flops, nbytes):
    return pl.CostEstimate(flops=flops, bytes_accessed=nbytes, transcendentals=0)


def pack_kernel(chips, core_ref, obs_ref, prior_ref, keep_ref, give_ref):
    sub = obs_ref.shape[0] // (2 * chips)
    evo = prior_ref.shape[0]
    for m in range(chips):
        for side, out_ref in enumerate((keep_ref, give_ref)):
            start = pl.multiple_of((2 * m + jnp.bitwise_xor(core_ref[0], side)) * sub, LANES)
            out_ref[m, :sub] = obs_ref[pl.ds(start, sub)]
            for l in range(sub // LANES):
                value = prior_ref[:, pl.ds(pl.multiple_of(start + l * LANES, LANES), LANES)]
                high = value.astype(BF16)
                row = sub + l * 2 * evo
                out_ref[m, row : row + evo] = high
                out_ref[m, row + evo : row + 2 * evo] = (value - high.astype(F32)).astype(BF16)


def pack(core, obs, prior_t, n_col, spare):
    rows, width = obs.shape
    evo = prior_t.shape[0]
    sub = rows // n_col
    depth = sub + 2 * evo * sub // LANES
    chips = 4
    block = pl.BlockSpec((chips, depth, width), lambda i, _: (i, 0, 0))
    return pl.pallas_call(
        functools.partial(pack_kernel, chips),
        out_shape=[jax.ShapeDtypeStruct((n_col // 2, depth + more, width), BF16) for more in (0, spare)],
        grid_spec=pltpu.PrefetchScalarGridSpec(
            num_scalar_prefetch=1,
            grid=(n_col // 2 // chips,),
            in_specs=[
                pl.BlockSpec((2 * chips * sub, width), lambda i, _: (i, 0)),
                pl.BlockSpec((evo, 2 * chips * sub), lambda i, _: (0, i)),
            ],
            out_specs=[block] * 2,
        ),
        cost_estimate=cost(0, 2 * 2 * n_col * depth * width),
    )(core, obs, prior_t)


def join_kernel(depth, got_ref, picked_ref, out_ref, tiles, sems):
    evo, count = picked_ref.shape
    for l in range(count // LANES):
        tiles[l * evo : (l + 1) * evo] = picked_ref[:, l * LANES : (l + 1) * LANES]
    copies = [
        pltpu.make_async_copy(tiles, out_ref.at[m, pl.ds(depth, tiles.shape[0])], sems.at[m])
        for m in range(out_ref.shape[0])
    ]
    for copy in copies:
        copy.start()
    for copy in copies:
        copy.wait()


def join(got, picked, depth):
    chips, full, width = got.shape
    anywhere = pl.BlockSpec(memory_space=pl.ANY)
    return pl.pallas_call(
        functools.partial(join_kernel, depth),
        out_shape=jax.ShapeDtypeStruct(got.shape, BF16),
        in_specs=[anywhere] + whole(1),
        out_specs=anywhere,
        scratch_shapes=[pltpu.VMEM((full - depth, width), BF16), pltpu.SemaphoreType.DMA((chips,))],
        input_output_aliases={0: 0},
        cost_estimate=cost(0, 2 * chips * (full - depth) * width),
    )(got, picked)


def pick_kernel(first_ref, idx_ref, sky_ref, out_ref):
    evo, rows = sky_ref.shape
    groups = rows // WIDE
    local = idx_ref[...] - first_ref[0]
    place = lax.broadcasted_iota(jnp.int32, (WIDE, local.shape[1]), 0)
    onehot = jnp.where(place == (local & (WIDE - 1)), 1.0, 0.0).astype(BF16)
    group = lax.shift_right_arithmetic(local, WIDE.bit_length() - 1)
    total = jnp.zeros(out_ref.shape, F32)
    step = 16
    for start in range(0, groups, step):
        block = jnp.concatenate(
            [sky_ref[:, g * WIDE : (g + 1) * WIDE] for g in range(start, start + step)], axis=0
        )
        found = jnp.dot(block, onehot, preferred_element_type=F32)
        for g in range(step):
            total = total + jnp.where(group == start + g, found[g * evo : (g + 1) * evo], 0.0)
    out_ref[...] = total.astype(BF16)


def pick(first, idx, sky):
    evo, rows = sky.shape
    count = idx.shape[1]
    tile = 1024
    return pl.pallas_call(
        pick_kernel,
        out_shape=jax.ShapeDtypeStruct((evo, count), BF16),
        grid_spec=pltpu.PrefetchScalarGridSpec(
            num_scalar_prefetch=1,
            grid=(count // tile,),
            in_specs=[
                pl.BlockSpec((1, tile), lambda i, _: (0, i)),
                pl.BlockSpec((evo, rows), lambda i, _: (0, 0)),
            ],
            out_specs=pl.BlockSpec((evo, tile), lambda i, _: (0, i)),
        ),
        cost_estimate=cost(2 * evo * rows * count, 2 * evo * rows + 2 * evo * count),
    )(first, idx, sky)


def main_kernel(
    me_ref, near_ref, far_ref, other_ref, apod_ref, proj_ref, p_own, p_other, s_own, s_other, panel, weighted
):
    chips, evo, _ = p_own.shape
    prows, sub = proj_ref.shape
    me = me_ref[0]
    core = me % 2
    half = chips * evo
    depth = near_ref.shape[1]
    for k in range(chips):
        for side in range(2):
            tile = (2 * k + jnp.bitwise_xor(core, side)) * evo
            lanes = slice((2 * k + side) * LANES, (2 * k + side + 1) * LANES)
            for m in range(chips):
                panel[m * evo : (m + 1) * evo, lanes] = far_ref[m, pl.ds(pl.multiple_of(depth + tile, evo), evo)]
                panel[half + m * evo : half + (m + 1) * evo, lanes] = other_ref[
                    m, pl.ds(pl.multiple_of(tile, evo), evo)
                ]
    for n in range(sub // WIDE):
        rows = slice(n * WIDE, (n + 1) * WIDE)
        added = jnp.zeros((2 * half, WIDE), F32)
        for k in range(chips):
            obs = jnp.concatenate([near_ref[k, rows], far_ref[k, rows]], axis=1)
            added += lax.dot_general(
                panel[:, k * WIDE : (k + 1) * WIDE], obs, NT, preferred_element_type=F32
            )
        s_own[:, :, rows] = added[:half].astype(BF16).reshape(chips, evo, WIDE)
        s_other[:, :, rows] = added[half:].astype(BF16).reshape(chips, evo, WIDE)
        for l in range(WIDE // LANES):
            block = n * (WIDE // LANES) + l
            row = sub + block * 2 * evo
            prior = jnp.concatenate(
                [
                    ref[m, row : row + evo].astype(F32) + ref[m, row + evo : row + 2 * evo].astype(F32)
                    for ref in (near_ref, far_ref)
                    for m in range(chips)
                ],
                axis=0,
            )
            weight = apod_ref[pl.ds(me * (sub // LANES) + block, 1), :]
            value = weight * (prior + added[:, l * LANES : (l + 1) * LANES])
            weighted[:, block * LANES : (block + 1) * LANES] = value.astype(BF16)
    for n in range(prows // WIDE):
        cols = slice(n * WIDE, (n + 1) * WIDE)
        part = lax.dot_general(weighted[...], proj_ref[cols], NT, preferred_element_type=F32)
        p_own[:, :, cols] = part[:half].reshape(chips, evo, WIDE)
        p_other[:, :, cols] = part[half:].astype(BF16).reshape(chips, evo, WIDE)


def main_step(me, near, far, other, apod, proj, evo, count):
    chips = near.shape[0]
    prows, sub = proj.shape
    total = 2 * chips * evo
    return pl.pallas_call(
        main_kernel,
        out_shape=(
            jax.ShapeDtypeStruct((chips, evo, prows), F32),
            jax.ShapeDtypeStruct((chips, evo, prows), BF16),
            jax.ShapeDtypeStruct((chips, evo, sub), BF16),
            jax.ShapeDtypeStruct((chips, evo, sub), BF16),
        ),
        in_specs=[pl.BlockSpec(memory_space=pltpu.SMEM)] + whole(5),
        out_specs=tuple(whole(4)),
        scratch_shapes=[pltpu.VMEM((total, count), BF16), pltpu.VMEM((total, sub), BF16)],
        compiler_params=pltpu.CompilerParams(vmem_limit_bytes=28 * MIB),
        cost_estimate=cost(2 * total * sub * (count + prows), 4 * near.size + 2 * proj.size + 4 * total * prows),
    )(me, near, far, other, apod, proj)


def home_kernel(p_own, p_got, s_own, s_got, out_ref):
    prows, sub = p_own.shape[2], s_own.shape[2]
    out_ref[:, :, :prows] = (p_own[...] + p_got[...].astype(F32)).astype(BF16)
    out_ref[:, :, prows : prows + sub] = s_own[...]
    out_ref[:, :, prows + sub :] = s_got[...]


def sum_kernel(msg_ref, out_ref):
    width = out_ref.shape[2]
    for n in range(out_ref.shape[0]):
        out_ref[n] = jnp.sum(msg_ref[:, :, n * width : (n + 1) * width].astype(F32), axis=0)


def add_kernel(prows, core_ref, msg_ref, prior_ref, out_ref):
    chips = msg_ref.shape[0]
    sub = prior_ref.shape[1] // (2 * chips)
    core = core_ref[0]
    for m in range(chips):
        for b in range(2):
            at = pl.ds(pl.multiple_of((2 * m + jnp.bitwise_xor(core, b)) * sub, LANES), sub)
            came = msg_ref[m, :, prows + b * sub : prows + (b + 1) * sub].astype(F32)
            out_ref[:, at] = prior_ref[:, at] + came


def add_up(x, n_row):
    ring = n_row // 2

    def turn(y, by):
        return lax.ppermute(
            y, "row", [(h * ring + z, h * ring + (z + by) % ring) for h in range(2) for z in range(ring)]
        )

    below, above = turn(x, 1), turn(x, -1)
    two = x + above
    three = two + below
    x = three + turn(three, -3) + turn(two, 3)
    return x + swap(x, "row", ring, n_row)


def swap(x, axis, bits, n):
    return lax.ppermute(x, axis, [(i, i ^ bits) for i in range(n)])


def on_device(n_row, n_col, obs, skies, idx, prior, apod, proj):
    rows_blk, evo = skies.shape
    sub = rows_blk // n_col
    count = idx.shape[0]
    prows = proj.shape[0]
    chips = n_col // 2
    prior_t = prior.T
    me = lax.axis_index("col").astype(jnp.int32)
    core = (me % 2).reshape(1)
    first = (lax.axis_index("row") * rows_blk).astype(jnp.int32)
    same = [[2 * m + b for m in range(chips)] for b in range(2)]
    to_chips = functools.partial(
        lax.all_to_all, axis_name="col", split_axis=0, concat_axis=0, tiled=True, axis_index_groups=same
    )
    keep, give = pack(core, obs, prior_t, n_col, count * evo // LANES)
    keep, give, idx = lax.optimization_barrier((keep, give, idx))
    near_rows = to_chips(keep)
    picked = pick(first.reshape(1), idx.reshape(1, count), skies.T)
    got = swap(give, "col", 1, n_col)
    picked = add_up(picked, n_row)
    joined = join(got, picked, keep.shape[1])
    near_rows, joined = lax.optimization_barrier((near_rows, joined))
    far_rows = to_chips(joined)
    other = swap(far_rows[:, keep.shape[1] :], "col", 1, n_col)

    p_own, p_other, s_own, s_other = main_step(
        me.reshape(1), near_rows, far_rows, other, apod.reshape(rows_blk // LANES, LANES), proj, evo, count
    )
    p_got = swap(p_other, "col", 1, n_col)
    s_got = swap(s_other, "col", 1, n_col)
    home = pl.pallas_call(
        home_kernel,
        out_shape=jax.ShapeDtypeStruct((chips, evo, prows + 2 * sub), BF16),
        in_specs=whole(4),
        out_specs=whole(1)[0],
        compiler_params=pltpu.CompilerParams(vmem_limit_bytes=16 * MIB),
        cost_estimate=cost(p_own.size, 10 * p_own.size),
    )(p_own, p_got, s_own, s_got)
    home = to_chips(home)
    share = pl.pallas_call(
        sum_kernel,
        out_shape=jax.ShapeDtypeStruct((n_row, evo, prows // n_row), F32),
        grid=(1,),
        in_specs=[pl.BlockSpec((chips, evo, prows), lambda i: (0, 0, 0))],
        out_specs=pl.BlockSpec((n_row, evo, prows // n_row), lambda i: (0, 0, 0)),
        cost_estimate=cost(home.size, 2 * home.size),
    )(home)
    share = lax.all_to_all(share, "row", 0, 0, tiled=True)
    projection = share.sum(0).T
    reobserved = pl.pallas_call(
        functools.partial(add_kernel, prows),
        out_shape=jax.ShapeDtypeStruct((evo, rows_blk), F32),
        in_specs=[pl.BlockSpec(memory_space=pltpu.SMEM)] + whole(2),
        out_specs=whole(1)[0],
        cost_estimate=cost(prior.size, 10 * prior.size),
    )(core, home, prior_t).T
    return reobserved, projection


def solution(mesh):
    n_row, n_col = mesh.shape["row"], mesh.shape["col"]
    return jax.shard_map(
        functools.partial(on_device, n_row, n_col),
        mesh=mesh,
        in_specs=(P("row", "col"), P("row", "col"), P(), P("row", "col"), P("row"), P(None, ("row", "col"))),
        out_specs=(P("row", "col"), P("row", "col")),
        check_vma=False,
    )
```
